32 devices in a mesh: grp: 2 (over y), tile: 16 (over z, x, core).
Axes of the slice: x: 2, y: 2, z: 4, core: 2. Of those that a mesh axis runs over, the one named last changes fastest.
Arguments:
- fields: bfloat16 [6, 128, 128, 256], P('grp', 'tile'), parts along dimension 0, may hold values from -6 to 6
- seam_tile: int32 [3, 16, 2], P(None, 'tile'), may hold values from 0 to 47, as said below
- seam_code: int32 [3, 16, 2], P(None, 'tile'), may hold values from 0 to 3
- encoder_weight: bfloat16 [3, 3, 256, 256], replicated, may hold values from -0.125 to 0.125
- encoder_bias: float32 [256], replicated, may hold values from -3 to 3
- middle_weight: bfloat16 [3, 3, 256, 256], replicated, may hold values from -0.125 to 0.125
- middle_bias: float32 [256], replicated, may hold values from -3 to 3
- upconv_weight: bfloat16 [2, 2, 256, 256], replicated, may hold values from -0.375 to 0.375
- upconv_bias: float32 [256], replicated, may hold values from -3 to 3
- decoder_weight: bfloat16 [3, 3, 512, 256], replicated, may hold values from -0.09375 to 0.09375
- decoder_offset_bias: float32 [256], replicated, may hold values from -3 to 3
Outputs:
- decoded: bfloat16 [6, 128, 128, 256], P('grp', 'tile'), parts along dimension 0
The draws below stay inside these ranges and needn't reach their ends.
There are 2 independent parts, one for each index of `grp`. The reference program is written for one: setup_inputs(seed, part) draws one part's arguments, and reference() takes and returns one part's arrays. A program takes and returns all parts, laid end to end along the dimension named above; an argument that names none is the same for every part. Nothing has to cross between parts.
Inputs may be any that keep to these rules, and one draw needn't show every extreme that they name: `seam_tile`: for each side, the 12 faces (cycle, face) name 12 different partner faces; all 4 tiles of one face side share the partner face and the code, and strip s names the tile of strip s of the partner face, or of strip 4 - 1 - s where the code is 2 or more.
All inputs are finite; a program needn't handle non-finite values.
Results may differ from the reference program's by a relative error of at most 0.0048.
Values may be sent and summed in bfloat16 or wider, within the bound.
A program may use at most 128 MiB of HBM per device.

```python
import jax
import jax.numpy as jnp

C = 256
COLS = 128
TILES = 16
STRIPS = 4
ROWS = 128


def seam_layout(key):
    base = jax.random.fold_in(key, 7)
    key_left, key_right, key_code = jax.random.split(base, 3)
    order_left = jax.random.permutation(key_left, 12)
    order_right = jax.random.permutation(key_right, 12)
    partner_face = jnp.stack([order_left, order_right], axis=-1).reshape(3, 4, 1, 2).astype(jnp.int32)
    code_order = jax.random.permutation(key_code, 24)
    face_code = (code_order % 4).reshape(3, 4, 1, 2).astype(jnp.int32)
    strip_index = jnp.arange(STRIPS, dtype=jnp.int32).reshape(1, 1, STRIPS, 1)
    partner_strip = jnp.where(face_code >= 2, STRIPS - 1 - strip_index, strip_index)
    partner_cycle = partner_face // 4
    partner_in_cycle = partner_face % 4
    partner_place = (partner_in_cycle * STRIPS + partner_strip - STRIPS // 2) % TILES
    adjacent_tile = partner_cycle * TILES + partner_place
    seam_codes = jnp.broadcast_to(face_code, (3, 4, STRIPS, 2))
    adjacent_tile = jnp.roll(adjacent_tile.reshape(3, TILES, 2), -(STRIPS // 2), axis=1)
    seam_codes = jnp.roll(seam_codes.reshape(3, TILES, 2), -(STRIPS // 2), axis=1)
    return (adjacent_tile.astype(jnp.int32), seam_codes.astype(jnp.int32))


def draw_seam_tile(key, part):
    return seam_layout(key)[0]


def draw_seam_code(key, part):
    return seam_layout(key)[1]


def level_of(rng, dims, shards, smallest, high):
    factor_of = 1.0
    for axis_at, blocks in shards:
        steps = jax.random.uniform(jax.random.fold_in(jax.random.fold_in(rng, 6), axis_at), (blocks,), jnp.float32, smallest / len(shards), high / len(shards))
        factor_of = factor_of * jnp.repeat(jnp.exp(steps), dims[axis_at] // blocks).reshape((-1,) + (1,) * (len(dims) - 1 - axis_at))
    return factor_of


def bell_draw(rng, shape, spread, limit, shards=(), kind=jnp.bfloat16):
    entries = jax.random.normal(rng, shape, jnp.float32) * spread
    if len(shards) > 0:
        entries = level_of(rng, shape, shards, -0.22, 0.18) * entries
    return jnp.clip(entries, min=-limit, max=limit).astype(kind)


def setup_inputs(seed: int = 0, part: int = 0) -> dict:
    seeds = jax.random.split(jax.random.key(seed), 12)
    part_splits = jax.random.split(jax.random.fold_in(seeds[11], part), 12)
    fields = bell_draw(part_splits[0], (3, ROWS, COLS, C), 1.0, 6.0, ((1, 16),))
    seam_tile = draw_seam_tile(jax.random.fold_in(seeds[11], 71), part)
    seam_code = draw_seam_code(jax.random.fold_in(seeds[11], 71), part)
    encoder_weight = bell_draw(seeds[3], (3, 3, C, C), (9 * C) ** -0.5, 0.125)
    encoder_bias = bell_draw(seeds[4], (C,), 0.5, 3.0, (), jnp.float32)
    middle_weight = bell_draw(seeds[5], (3, 3, C, C), (9 * C) ** -0.5, 0.125)
    middle_bias = bell_draw(seeds[6], (C,), 0.5, 3.0, (), jnp.float32)
    upconv_weight = bell_draw(seeds[7], (2, 2, C, C), C ** -0.5, 0.375)
    upconv_bias = bell_draw(seeds[8], (C,), 0.5, 3.0, (), jnp.float32)
    decoder_weight = bell_draw(seeds[9], (3, 3, 2 * C, C), (18 * C) ** -0.5, 0.09375)
    decoder_offset_bias = bell_draw(seeds[10], (C,), 0.5, 3.0, (), jnp.float32)
    return dict(fields=fields, seam_tile=seam_tile, seam_code=seam_code, encoder_weight=encoder_weight, encoder_bias=encoder_bias, middle_weight=middle_weight, middle_bias=middle_bias, upconv_weight=upconv_weight, upconv_bias=upconv_bias, decoder_weight=decoder_weight, decoder_offset_bias=decoder_offset_bias)


def gelu_tanh(values):
    return jax.nn.gelu(values, approximate=True)


def blank_edge_rows(extended, top_face, bottom_face):
    upper_row = extended[..., :1, :, :]
    lower_row = extended[..., -1:, :, :]
    upper_row = jnp.where(top_face, jnp.zeros_like(upper_row), upper_row)
    lower_row = jnp.where(bottom_face, jnp.zeros_like(lower_row), lower_row)
    return jnp.concatenate([upper_row, extended[..., 1:-1, :, :], lower_row], axis=-3)


def boundary_columns(extended):
    return jnp.stack([extended[..., :, 0, :], extended[..., :, -1, :]], axis=-3)


def pick_partner(flattened, partners, seam_codes):
    chosen = flattened[partners]
    column_bit = (seam_codes % 2)[..., None, None]
    single = jnp.where(column_bit == 0, chosen[..., 0, :, :], chosen[..., 1, :, :])
    mirror_flag = (seam_codes // 2)[..., None, None]
    return jnp.where(mirror_flag == 1, single[..., ::-1, :], single)


def attach_columns(extended, picked):
    left_col = picked[..., 0, :, :][..., :, None, :]
    right_col = picked[..., 1, :, :][..., :, None, :]
    return jnp.concatenate([left_col, extended, right_col], axis=-2)


def convolve(padded, weight, bias):
    leading = padded.shape[:-3]
    rows_out = padded.shape[-3] - 2
    cols_out = padded.shape[-2] - 2
    chans_in = padded.shape[-1]
    chans_out = weight.shape[-1]
    accumulated = jnp.zeros(leading + (rows_out, cols_out, chans_out), jnp.float32)
    for row_tap in range(3):
        for col_tap in range(3):
            window = padded[..., row_tap:row_tap + rows_out, col_tap:col_tap + cols_out, :]
            product = jnp.dot(window.reshape(-1, chans_in), weight[row_tap, col_tap], preferred_element_type=jnp.float32)
            accumulated = accumulated + product.reshape(accumulated.shape)
    return accumulated + bias


def coarsen_grid(sphere_map):
    leading = sphere_map.shape[:-3]
    rows_in, cols_in, chans_in = sphere_map.shape[-3:]
    values = sphere_map.astype(jnp.float32).reshape(leading + (rows_in // 2, 2, cols_in // 2, 2, chans_in))
    return jnp.mean(values, axis=(-4, -2)).astype(jnp.bfloat16)


def upsample(coarse, weight, bias):
    leading = coarse.shape[:-3]
    rows_in, cols_in, chans_in = coarse.shape[-3:]
    chans_out = weight.shape[-1]
    flattened = coarse.reshape(-1, chans_in)
    phases = []
    for row_phase in range(2):
        phase_row = []
        for col_phase in range(2):
            product = jnp.dot(flattened, weight[row_phase, col_phase], preferred_element_type=jnp.float32)
            phase_row.append(product.reshape(leading + (rows_in, cols_in, chans_out)))
        phases.append(jnp.stack(phase_row, axis=-2).reshape(leading + (rows_in, 2 * cols_in, chans_out)))
    full = jnp.stack(phases, axis=-3).reshape(leading + (2 * rows_in, 2 * cols_in, chans_out))
    return (full + bias).astype(jnp.bfloat16)


def pad_field(sphere_map, partners, seam_codes):
    rows_in = sphere_map.shape[1] // TILES
    tiles = sphere_map.reshape(3, TILES, rows_in, sphere_map.shape[2], sphere_map.shape[3])
    upper_row = jnp.roll(tiles[:, :, -1:], 1, axis=1)
    lower_row = jnp.roll(tiles[:, :, :1], -1, axis=1)
    extended = jnp.concatenate([upper_row, tiles, lower_row], axis=2)
    strip_index = ((jnp.arange(TILES, dtype=jnp.int32) + STRIPS // 2) % STRIPS).reshape(1, TILES, 1, 1, 1)
    extended = blank_edge_rows(extended, strip_index == 0, strip_index == STRIPS - 1)
    edges = boundary_columns(extended)
    flattened = edges.reshape((3 * TILES,) + edges.shape[2:])
    return attach_columns(extended, pick_partner(flattened, partners, seam_codes))


def reference(fields, seam_tile, seam_code, encoder_weight, encoder_bias, middle_weight, middle_bias, upconv_weight, upconv_bias, decoder_weight, decoder_offset_bias):
    padded = pad_field(fields, seam_tile, seam_code)
    shortcut_map = gelu_tanh(convolve(padded, encoder_weight, encoder_bias)).astype(jnp.bfloat16)
    shortcut_map = shortcut_map.reshape(3, ROWS, COLS, C)
    averaged_map = coarsen_grid(shortcut_map)
    padded = pad_field(averaged_map, seam_tile, seam_code)
    coarse = gelu_tanh(convolve(padded, middle_weight, middle_bias)).astype(jnp.bfloat16)
    coarse = coarse.reshape(3, ROWS // 2, COLS // 2, C)
    upsampled = upsample(coarse, upconv_weight, upconv_bias)
    joined = jnp.concatenate([upsampled, shortcut_map], axis=-1)
    padded = pad_field(joined, seam_tile, seam_code)
    decoded = convolve(padded, decoder_weight, decoder_offset_bias).astype(jnp.bfloat16)
    return decoded.reshape(3, ROWS, COLS, C)
```

```python
import functools

import jax
import jax.numpy as jnp
from jax import lax
from jax.experimental import pallas as pl
from jax.experimental.pallas import tpu as pltpu
from jax.sharding import PartitionSpec as P

F32 = jnp.float32
BF16 = jnp.bfloat16
FACES = 4


def gelu_tanh(x):
    return 0.5 * x * (1.0 + jnp.tanh(0.7978845608 * (x + 0.044715 * (x * x * x))))


def kernel(
    tiles,
    seam_tile,
    seam_code,
    fields_hbm,
    enc_w_hbm,
    mid_w_hbm,
    up_w_hbm,
    dec_w_hbm,
    enc_b,
    mid_b,
    up_b,
    dec_b,
    out,
    fields,
    enc_w,
    mid_w,
    up_w,
    dec_w,
    x_enc,
    x_skip,
    x_pool,
    x_up,
    acc_enc,
    acc_dec,
    coarse,
    fine,
    pair,
    corner_tmp,
    edge_tmp,
    seam_tmp,
    corner_src,
    corner_dst,
    halo,
    halo_pool,
    edges,
    edges_pool,
    recv_enc,
    recv_skip,
    recv_up,
    recv_pool,
    load_sem,
    send_sem,
    recv_sem,
):
    cycles, h, cols, ch = fields.shape
    hc, cc = h // 2, cols // 2
    strips = tiles // FACES
    me = lax.axis_index("tile")
    place = lax.rem(me + strips // 2, tiles)
    face = place // strips
    strip = place - face * strips
    top_face = strip == 0
    bottom_face = strip == strips - 1
    up_tile = lax.rem(me + tiles - 1, tiles)
    down_tile = lax.rem(me + 1, tiles)

    def tile_of(f, s):
        return lax.rem(f * strips + s + tiles - strips // 2, tiles)

    peers = []
    for kind in range(2):
        s = strip if kind == 0 else strips - 1 - strip
        for j in range(1 - kind, FACES):
            f = lax.rem(face + j, FACES)
            peers.append((kind, f, tile_of(f, s)))

    loads = []
    for k, (src, dst) in enumerate(
        ((fields_hbm, fields), (enc_w_hbm, enc_w), (dec_w_hbm, dec_w), (mid_w_hbm, mid_w), (up_w_hbm, up_w))
    ):
        copy = pltpu.make_async_copy(src, dst, load_sem.at[k])
        copy.start()
        loads.append(copy)

    barrier = pltpu.get_barrier_semaphore()
    targets = [up_tile, down_tile] + [peer for _, _, peer in peers]
    for target in targets:
        pl.semaphore_signal(barrier, inc=1, device_id={"tile": target})
    pl.semaphore_wait(barrier, len(targets))

    def remote(src, dst, e, send_at, recv_at, target):
        return pltpu.make_async_remote_copy(
            src_ref=src,
            dst_ref=dst,
            send_sem=send_sem.at[e, send_at],
            recv_sem=recv_sem.at[e, recv_at],
            device_id={"tile": target},
        )

    def spread(x, i, r, value):
        width = value.shape[0]
        at = lax.broadcasted_iota(jnp.int32, value.shape, 0)
        left = jnp.where(at == 0, 0.0, pltpu.roll(value, 1, 0))
        right = jnp.where(at == width - 1, 0.0, pltpu.roll(value, width - 1, 0))
        x[i, r, :, 0:ch] = left.astype(BF16)
        x[i, r, :, ch : 2 * ch] = value.astype(BF16)
        x[i, r, :, 2 * ch : 3 * ch] = right.astype(BF16)

    class Exchange:
        def __init__(self, e, x, halo_ref, edge_ref, recv_ref):
            self.e, self.x, self.halo, self.edges, self.recv = e, x, halo_ref, edge_ref, recv_ref
            self.rows = x.shape[0] - 2
            self.width = x.shape[2]

        def end_pixels(self, i, r):
            head = self.x[i, r, 0:16, ch : 2 * ch].astype(F32)[0:1]
            tail = self.x[i, r, self.width - 16 : self.width, ch : 2 * ch].astype(F32)[15:16]
            return head, tail

        def send_rows(self):
            e, x, rows = self.e, self.x, self.rows
            for which, i in ((0, 1), (1, rows)):
                for r in range(cycles):
                    head, tail = self.end_pixels(i, r)
                    corner_tmp[e, which, 2 * r : 2 * r + 1, :] = head
                    corner_tmp[e, which, 2 * r + 1 : 2 * r + 2, :] = tail
                corner_src[e, which] = corner_tmp[e, which].astype(BF16)
            self.copies = [
                remote(corner_src.at[e, 1], corner_dst.at[e, 0], e, 0, 0, down_tile),
                remote(corner_src.at[e, 0], corner_dst.at[e, 1], e, 1, 1, up_tile),
                remote(x.at[rows, :, :, ch : 2 * ch], self.halo.at[0], e, 2, 2, down_tile),
                remote(x.at[1, :, :, ch : 2 * ch], self.halo.at[1], e, 3, 3, up_tile),
            ]
            for copy in self.copies:
                copy.start()

        def send_edges(self):
            e, rows = self.e, self.rows
            self.copies[0].wait_recv()
            self.copies[1].wait_recv()
            above = jnp.where(top_face, 0.0, corner_dst[e, 0].astype(F32))
            below = jnp.where(bottom_face, 0.0, corner_dst[e, 1].astype(F32))
            for r in range(cycles):
                for side in range(2):
                    k = 2 * r + side
                    edge_tmp[e, k, 0:1, :] = above[k : k + 1]
                    edge_tmp[e, k, rows + 1 : rows + 2, :] = below[k : k + 1]
                for i in range(rows):
                    for side, pixel in enumerate(self.end_pixels(i + 1, r)):
                        edge_tmp[e, 2 * r + side, i + 1 : i + 2, :] = pixel
            value = edge_tmp[e, :, 0 : rows + 2, :].astype(BF16)
            self.edges[...] = value
            self.recv[face] = value
            self.seams = [
                remote(
                    self.edges,
                    self.recv.at[kind * FACES + face],
                    e,
                    4 + kind * FACES + f,
                    4 + kind * FACES + face,
                    peer,
                )
                for kind, f, peer in peers
            ]
            for copy in self.seams:
                copy.start()

        def wait_rows(self):
            self.copies[2].wait_recv()
            self.copies[3].wait_recv()
            for r in range(cycles):
                above = jnp.where(top_face, 0.0, self.halo[0, r].astype(F32))
                spread(self.x, 0, r, above)
                below = jnp.where(bottom_face, 0.0, self.halo[1, r].astype(F32))
                spread(self.x, self.rows + 1, r, below)

        def seam_terms(self, weight_of):
            e, rows = self.e, self.rows
            for kind, f, peer in peers:
                slot = kind * FACES + f
                remote(self.edges, self.recv.at[slot], e, 4 + slot, 4 + slot, peer).wait_recv()
            for copy in self.copies + self.seams:
                copy.wait_send()
            terms = []
            for side in range(2):
                for r in range(cycles):
                    partner, code = seam_tile[r, side], seam_code[r, side]
                    cycle = partner // tiles
                    home = lax.rem(partner - cycle * tiles + strips // 2, tiles) // strips
                    mirrored = code >= 2
                    slot = jnp.where(mirrored, FACES, 0) + home
                    column = self.recv[slot, 2 * cycle + lax.rem(code, 2)].astype(F32)
                    for i in range(rows + 2):
                        seam_tmp[side, r, i : i + 1, :] = jnp.where(
                            mirrored, column[rows + 1 - i : rows + 2 - i], column[i : i + 1]
                        )
                taps = [
                    jnp.concatenate([seam_tmp[side, r, a : a + 8, :] for r in range(cycles)], axis=0).astype(BF16)
                    for a in range(3)
                ]
                term = jnp.zeros((8 * cycles, ch), F32)
                for a in range(3):
                    term = term + jnp.dot(taps[a], weight_of(a, 2 * side), preferred_element_type=F32)
                terms.append(term)
            return terms

        def add_seams(self, acc, weight_of):
            terms = self.seam_terms(weight_of)
            for side in range(2):
                j = 0 if side == 0 else self.width - 1
                for r in range(cycles):
                    for i in range(self.rows):
                        acc[i, r, j : j + 1, :] += terms[side][8 * r + i : 8 * r + i + 1]

    def conv_rows(x, start, count, weights):
        width = x.shape[2]
        taps = [x[pl.ds(start + a, count)].reshape(count * cycles * width, 3 * ch) for a in range(3)]
        product = jnp.dot(jnp.concatenate(taps, axis=1), weights(), preferred_element_type=F32)
        return product.reshape(count, cycles, width, ch)

    def enc_weights():
        return enc_w[...].reshape(9 * ch, ch)

    def mid_weights():
        return mid_w[...].reshape(9 * ch, ch)

    def dec_weights(part):
        def get():
            picked = [dec_w[a, b, part * ch : (part + 1) * ch, :] for a in range(3) for b in range(3)]
            return jnp.concatenate(picked, axis=0)

        return get

    def dec_tap(part):
        return lambda a, b: dec_w[a, b, part * ch : (part + 1) * ch, :]

    loads[0].wait()

    @pl.loop(0, h)
    def _(i):
        for r in range(cycles):
            spread(x_enc, i + 1, r, fields[r, i].astype(F32))

    enc = Exchange(0, x_enc, halo.at[0], edges.at[0], recv_enc)
    enc.send_rows()
    loads[1].wait()

    def inner_rows(x, acc, weights, lo, hi, add):
        @pl.loop(lo, hi)
        def _(k):
            start = 1 + 2 * k
            value = conv_rows(x, start, 2, weights)
            if add:
                acc[pl.ds(start, 2)] += value
            else:
                acc[pl.ds(start, 2)] = value

    inner = (h - 2) // 2
    inner_rows(x_enc, acc_enc, enc_weights, 0, 1, False)
    enc.send_edges()
    inner_rows(x_enc, acc_enc, enc_weights, 1, inner, False)
    enc.wait_rows()

    def outer_rows(x, acc, weights, add):
        @pl.loop(0, 2)
        def _(k):
            i = k * (h - 1)
            value = conv_rows(x, i, 1, weights)
            if add:
                acc[pl.ds(i, 1)] += value
            else:
                acc[pl.ds(i, 1)] = value

    outer_rows(x_enc, acc_enc, enc_weights, False)
    enc.add_seams(acc_enc, lambda a, b: enc_w[a, b])

    @pl.loop(0, hc)
    def _(q):
        for r in range(cycles):
            total = None
            for a in range(2):
                value = gelu_tanh(acc_enc[2 * q + a, r] + enc_b[...]).astype(BF16).astype(F32)
                spread(x_skip, 2 * q + a + 1, r, value)
                total = value if total is None else total + value
            halves = []
            for k in range(ch // 128):
                pair[r, k] = total[:, k * 128 : (k + 1) * 128]
                even = pair[r, k, pl.ds(0, cc, stride=2), :]
                odd = pair[r, k, pl.ds(1, cc, stride=2), :]
                halves.append((even + odd) * 0.25)
            spread(x_pool, q + 1, r, jnp.concatenate(halves, axis=1).astype(BF16).astype(F32))

    pool = Exchange(1, x_pool, halo_pool, edges_pool, recv_pool)
    skip = Exchange(2, x_skip, halo.at[1], edges.at[1], recv_skip)
    pool.send_rows()
    loads[2].wait()
    inner_rows(x_skip, acc_dec, dec_weights(1), 0, 1, False)
    pool.send_edges()
    skip.send_rows()
    inner_rows(x_skip, acc_dec, dec_weights(1), 1, inner, False)
    skip.send_edges()

    loads[3].wait()
    loads[4].wait()
    pool.wait_rows()

    acc_mid = acc_enc.at[0:hc, :, 0:cc, :]

    @pl.loop(0, hc // 2)
    def _(k):
        acc_enc[pl.ds(2 * k, 2), :, 0:cc, :] = conv_rows(x_pool, 2 * k, 2, mid_weights)

    pool.add_seams(acc_mid, lambda a, b: mid_w[a, b])

    @pl.loop(0, hc)
    def _(q):
        for r in range(cycles):
            value = gelu_tanh(acc_enc[q, r, 0:cc, :] + mid_b[...])
            coarse[q, r] = value.astype(BF16)

    @pl.loop(0, hc)
    def _(q):
        lhs = coarse[q].reshape(cycles * cc, ch)
        for a in range(2):
            for b in range(2):
                value = jnp.dot(lhs, up_w[a, b], preferred_element_type=F32) + up_b[...]
                for r in range(cycles):
                    for k in range(ch // 128):
                        fine[a, r, k, pl.ds(b, cc, stride=2), :] = value[
                            r * cc : (r + 1) * cc, k * 128 : (k + 1) * 128
                        ]
            for r in range(cycles):
                row = jnp.concatenate([fine[a, r, k] for k in range(ch // 128)], axis=1)
                spread(x_up, 2 * q + a + 1, r, row.astype(BF16).astype(F32))

    up = Exchange(3, x_up, halo.at[2], edges.at[2], recv_up)
    up.send_rows()
    skip.wait_rows()
    outer_rows(x_skip, acc_dec, dec_weights(1), False)
    up.send_edges()
    inner_rows(x_up, acc_dec, dec_weights(0), 0, inner, True)
    skip.add_seams(acc_dec, dec_tap(1))
    up.wait_rows()
    outer_rows(x_up, acc_dec, dec_weights(0), True)
    up.add_seams(acc_dec, dec_tap(0))

    @pl.loop(0, h)
    def _(i):
        for r in range(cycles):
            out[r, i] = (acc_dec[i, r] + dec_b[...]).astype(BF16)


def solution(mesh):
    tiles = mesh.shape["tile"]

    def on_device(fields, seam_tile, seam_code, enc_w, enc_b, mid_w, mid_b, up_w, up_b, dec_w, dec_b):
        cycles, h, cols, ch = fields.shape
        hc, cc = h // 2, cols // 2
        vmem = pl.BlockSpec(memory_space=pltpu.VMEM)
        smem = pl.BlockSpec(memory_space=pltpu.SMEM)
        hbm = pl.BlockSpec(memory_space=pl.ANY)
        ends = 2 * cycles
        slots = 2 * FACES
        return pl.pallas_call(
            functools.partial(kernel, tiles),
            out_shape=jax.ShapeDtypeStruct(fields.shape, BF16),
            in_specs=[smem, smem] + [hbm] * 5 + [vmem] * 4,
            out_specs=vmem,
            scratch_shapes=[
                pltpu.VMEM(fields.shape, BF16),
                pltpu.VMEM(enc_w.shape, BF16),
                pltpu.VMEM(mid_w.shape, BF16),
                pltpu.VMEM(up_w.shape, BF16),
                pltpu.VMEM(dec_w.shape, BF16),
                pltpu.VMEM((h + 2, cycles, cols, 3 * ch), BF16),
                pltpu.VMEM((h + 2, cycles, cols, 3 * ch), BF16),
                pltpu.VMEM((hc + 2, cycles, cc, 3 * ch), BF16),
                pltpu.VMEM((h + 2, cycles, cols, 3 * ch), BF16),
                pltpu.VMEM((h, cycles, cols, ch), F32),
                pltpu.VMEM((h, cycles, cols, ch), F32),
                pltpu.VMEM((hc, cycles, cc, ch), BF16),
                pltpu.VMEM((2, cycles, ch // 128, cols, 128), F32),
                pltpu.VMEM((cycles, ch // 128, cols, 128), F32),
                pltpu.VMEM((4, 2, 8, ch), F32),
                pltpu.VMEM((4, ends, 16, ch), F32),
                pltpu.VMEM((2, cycles, 16, ch), F32),
                pltpu.VMEM((4, 2, 8, ch), BF16),
                pltpu.VMEM((4, 2, 8, ch), BF16),
                pltpu.VMEM((3, 2, cycles, cols, ch), BF16),
                pltpu.VMEM((2, cycles, cc, ch), BF16),
                pltpu.VMEM((3, ends, h + 2, ch), BF16),
                pltpu.VMEM((ends, hc + 2, ch), BF16),
                pltpu.VMEM((slots, ends, h + 2, ch), BF16),
                pltpu.VMEM((slots, ends, h + 2, ch), BF16),
                pltpu.VMEM((slots, ends, h + 2, ch), BF16),
                pltpu.VMEM((slots, ends, hc + 2, ch), BF16),
                pltpu.SemaphoreType.DMA((5,)),
                pltpu.SemaphoreType.DMA((4, 4 + slots)),
                pltpu.SemaphoreType.DMA((4, 4 + slots)),
            ],
            compiler_params=pltpu.CompilerParams(
                collective_id=0, has_side_effects=True, vmem_limit_bytes=60 * 1024 * 1024
            ),
        )(
            seam_tile.reshape(cycles, 2),
            seam_code.reshape(cycles, 2),
            fields,
            enc_w,
            mid_w,
            up_w,
            dec_w,
            enc_b.reshape(1, ch),
            mid_b.reshape(1, ch),
            up_b.reshape(1, ch),
            dec_b.reshape(1, ch),
        )

    return jax.shard_map(
        on_device,
        mesh=mesh,
        in_specs=(P("grp", "tile", None, None), P(None, "tile", None), P(None, "tile", None)) + (P(),) * 8,
        out_specs=P("grp", "tile", None, None),
        check_vma=False,
    )
```

```python
import functools

import jax
import jax.numpy as jnp
from jax import lax
from jax.experimental import pallas as pl
from jax.experimental.pallas import tpu as pltpu
from jax.sharding import PartitionSpec as P

F32 = jnp.float32
BF16 = jnp.bfloat16
FACES = 4


def gelu_tanh(x):
    return 0.5 * x * (1.0 + jnp.tanh(0.7978845608 * (x + 0.044715 * (x * x * x))))


def kernel(
    tiles,
    seam_tile,
    seam_code,
    fields_hbm,
    enc_w_hbm,
    mid_w_hbm,
    up_w_hbm,
    dec_w_hbm,
    enc_b,
    mid_b,
    up_b,
    dec_b,
    out,
    fields,
    enc_w,
    mid_w,
    up_w,
    dec_w,
    x_enc,
    x_skip,
    x_pool,
    x_up,
    acc_enc,
    acc_dec,
    coarse,
    fine,
    pair,
    corner_tmp,
    edge_tmp,
    seam_tmp,
    corner_src,
    corner_dst,
    corners,
    halo,
    halo_pool,
    edges,
    edges_pool,
    recv_enc,
    recv_skip,
    recv_up,
    recv_pool,
    corner_enc,
    corner_pool,
    corner_skip,
    corner_up,
    load_sem,
    send_sem,
    recv_sem,
):
    recv_corners = (corner_enc, corner_pool, corner_skip, corner_up)
    cycles, h, cols, ch = fields.shape
    hc, cc = h // 2, cols // 2
    strips = tiles // FACES
    me = lax.axis_index("tile")
    place = lax.rem(me + strips // 2, tiles)
    face = place // strips
    strip = place - face * strips
    top_face = strip == 0
    bottom_face = strip == strips - 1
    up_tile = lax.rem(me + tiles - 1, tiles)
    down_tile = lax.rem(me + 1, tiles)

    def tile_of(f, s):
        return lax.rem(f * strips + s + tiles - strips // 2, tiles)

    peers = []
    for kind in range(2):
        s = strip if kind == 0 else strips - 1 - strip
        for j in range(1 - kind, FACES):
            f = lax.rem(face + j, FACES)
            peers.append((kind, f, tile_of(f, s)))

    loads = []
    for k, (src, dst) in enumerate(
        ((fields_hbm, fields), (enc_w_hbm, enc_w), (dec_w_hbm, dec_w), (mid_w_hbm, mid_w), (up_w_hbm, up_w))
    ):
        copy = pltpu.make_async_copy(src, dst, load_sem.at[k])
        copy.start()
        loads.append(copy)

    barrier = pltpu.get_barrier_semaphore()
    targets = [up_tile, down_tile] + [peer for _, _, peer in peers]
    for target in targets:
        pl.semaphore_signal(barrier, inc=1, device_id={"tile": target})

    def remote(src, dst, e, send_at, recv_at, target):
        return pltpu.make_async_remote_copy(
            src_ref=src,
            dst_ref=dst,
            send_sem=send_sem.at[e, send_at],
            recv_sem=recv_sem.at[e, recv_at],
            device_id={"tile": target},
        )

    def spread(x, i, r, value):
        width = value.shape[0]
        at = lax.broadcasted_iota(jnp.int32, value.shape, 0)
        left = jnp.where(at == 0, 0.0, pltpu.roll(value, 1, 0))
        right = jnp.where(at == width - 1, 0.0, pltpu.roll(value, width - 1, 0))
        x[i, r, :, 0:ch] = left.astype(BF16)
        x[i, r, :, ch : 2 * ch] = value.astype(BF16)
        x[i, r, :, 2 * ch : 3 * ch] = right.astype(BF16)

    class Exchange:
        def __init__(self, e, x, halo_ref, edge_ref, recv_ref, source=None):
            self.e, self.x, self.halo, self.edges, self.recv = e, x, halo_ref, edge_ref, recv_ref
            self.rows = x.shape[0] - 2
            self.width = x.shape[2]
            self.source = source

        def row(self, i):
            if self.source is None:
                return self.x.at[i + 1, :, :, ch : 2 * ch]
            return self.source.at[:, i]

        def end_pixels(self, i, r):
            row = self.row(i)
            head = row[r, 0:16, :].astype(F32)[0:1]
            tail = row[r, self.width - 16 : self.width, :].astype(F32)[15:16]
            return head, tail

        def prepare(self):
            e, rows = self.e, self.rows
            for r in range(cycles):
                for i in range(rows):
                    for side, pixel in enumerate(self.end_pixels(i, r)):
                        k = 2 * r + side
                        edge_tmp[e, k, i : i + 1, :] = pixel
                        if i == 0:
                            corner_tmp[e, 0, k : k + 1, :] = pixel
                        if i == rows - 1:
                            corner_tmp[e, 1, k : k + 1, :] = pixel
            for which in range(2):
                corner_src[e, which] = corner_tmp[e, which].astype(BF16)
            value = edge_tmp[e, :, 0:rows, :].astype(BF16)
            self.edges[...] = value
            self.recv[face] = value

        def send(self):
            e, rows = self.e, self.rows
            self.copies = [
                remote(corner_src.at[e, 1], corner_dst.at[e, 0], e, 0, 0, down_tile),
                remote(corner_src.at[e, 0], corner_dst.at[e, 1], e, 1, 1, up_tile),
                remote(self.row(rows - 1), self.halo.at[0], e, 2, 2, down_tile),
                remote(self.row(0), self.halo.at[1], e, 3, 3, up_tile),
            ]
            self.seams = [
                remote(
                    self.edges,
                    self.recv.at[kind * FACES + face],
                    e,
                    4 + kind * FACES + f,
                    4 + kind * FACES + face,
                    peer,
                )
                for kind, f, peer in peers
            ]
            for copy in self.copies[0:2] + self.seams + self.copies[2:4]:
                copy.start()

        def relay(self):
            e = self.e
            self.copies[0].wait_recv()
            self.copies[1].wait_recv()
            above = jnp.where(top_face, 0.0, corner_dst[e, 0].astype(F32))
            below = jnp.where(bottom_face, 0.0, corner_dst[e, 1].astype(F32))
            value = jnp.concatenate([above, below], axis=0).astype(BF16)
            corners[e] = value
            self.recv_corner = recv_corners[e]
            self.recv_corner[face] = value
            self.relays = [
                remote(
                    corners.at[e],
                    self.recv_corner.at[kind * FACES + face],
                    e,
                    12 + kind * FACES + f,
                    12 + kind * FACES + face,
                    peer,
                )
                for kind, f, peer in peers
            ]
            for copy in self.relays:
                copy.start()

        def wait_rows(self):
            self.copies[2].wait_recv()
            self.copies[3].wait_recv()
            for r in range(cycles):
                above = jnp.where(top_face, 0.0, self.halo[0, r].astype(F32))
                spread(self.x, 0, r, above)
                below = jnp.where(bottom_face, 0.0, self.halo[1, r].astype(F32))
                spread(self.x, self.rows + 1, r, below)

        def wait_seams(self):
            e = self.e
            for kind, f, peer in peers:
                slot = kind * FACES + f
                remote(self.edges, self.recv.at[slot], e, 4 + slot, 4 + slot, peer).wait_recv()
                remote(
                    corners.at[e], self.recv_corner.at[slot], e, 12 + slot, 12 + slot, peer
                ).wait_recv()
            for copy in self.copies + self.seams + self.relays:
                copy.wait_send()

        def load_seams(self):
            rows = self.rows
            at = lax.broadcasted_iota(jnp.int32, (8, ch), 0)
            for side in range(2):
                for r in range(cycles):
                    partner, code = seam_tile[r, side], seam_code[r, side]
                    cycle = partner // tiles
                    home = lax.rem(partner - cycle * tiles + strips // 2, tiles) // strips
                    mirrored = code >= 2
                    slot = jnp.where(mirrored, FACES, 0) + home
                    k = 2 * cycle + lax.rem(code, 2)
                    column = self.recv[slot, k].astype(F32)
                    ends = self.recv_corner[slot].astype(F32)
                    above = jnp.sum(jnp.where(at == k, ends[0:8], 0.0), axis=0, keepdims=True)
                    below = jnp.sum(jnp.where(at == k, ends[8:16], 0.0), axis=0, keepdims=True)
                    seam_tmp[side, r, 0:1, :] = jnp.where(mirrored, below, above)
                    seam_tmp[side, r, rows + 1 : rows + 2, :] = jnp.where(mirrored, above, below)
                    for i in range(rows):
                        seam_tmp[side, r, i + 1 : i + 2, :] = jnp.where(
                            mirrored, column[rows - 1 - i : rows - i], column[i : i + 1]
                        )

        def add_seams(self, acc, weight_of):
            self.wait_seams()
            self.load_seams()
            for side in range(2):
                j = 0 if side == 0 else self.width - 1
                term = jnp.zeros((8 * cycles, ch), F32)
                for a in range(3):
                    tap = jnp.concatenate([seam_tmp[side, r, a : a + 8, :] for r in range(cycles)], axis=0)
                    term = term + jnp.dot(tap.astype(BF16), weight_of(a, 2 * side), preferred_element_type=F32)
                for r in range(cycles):
                    for i in range(self.rows):
                        acc[i, r, j : j + 1, :] += term[8 * r + i : 8 * r + i + 1]

    def conv_rows(x, start, count, weights):
        width = x.shape[2]
        taps = [x[pl.ds(start + a, count)].reshape(count * cycles * width, 3 * ch) for a in range(3)]
        product = jnp.dot(jnp.concatenate(taps, axis=1), weights(), preferred_element_type=F32)
        return product.reshape(count, cycles, width, ch)

    def enc_weights():
        return enc_w[...].reshape(9 * ch, ch)

    def mid_weights():
        return mid_w[...].reshape(9 * ch, ch)

    def dec_weights(part):
        def get():
            picked = [dec_w[a, b, part * ch : (part + 1) * ch, :] for a in range(3) for b in range(3)]
            return jnp.concatenate(picked, axis=0)

        return get

    def dec_tap(part):
        return lambda a, b: dec_w[a, b, part * ch : (part + 1) * ch, :]

    loads[0].wait()
    enc = Exchange(0, x_enc, halo.at[0], edges.at[0], recv_enc, fields)
    enc.prepare()
    pl.semaphore_wait(barrier, len(targets))
    enc.send()

    @pl.loop(0, h)
    def _(i):
        for r in range(cycles):
            spread(x_enc, i + 1, r, fields[r, i].astype(F32))

    loads[1].wait()

    def inner_rows(x, acc, weights, lo, hi, add):
        @pl.loop(lo, hi)
        def _(k):
            start = 1 + 2 * k
            value = conv_rows(x, start, 2, weights)
            if add:
                acc[pl.ds(start, 2)] += value
            else:
                acc[pl.ds(start, 2)] = value

    inner = (h - 2) // 2
    enc.relay()
    inner_rows(x_enc, acc_enc, enc_weights, 0, inner, False)
    enc.wait_rows()

    def outer_rows(x, acc, weights, add):
        @pl.loop(0, 2)
        def _(k):
            i = k * (h - 1)
            value = conv_rows(x, i, 1, weights)
            if add:
                acc[pl.ds(i, 1)] += value
            else:
                acc[pl.ds(i, 1)] = value

    outer_rows(x_enc, acc_enc, enc_weights, False)
    enc.add_seams(acc_enc, lambda a, b: enc_w[a, b])

    @pl.loop(0, hc)
    def _(q):
        for r in range(cycles):
            total = None
            for a in range(2):
                value = gelu_tanh(acc_enc[2 * q + a, r] + enc_b[...]).astype(BF16).astype(F32)
                spread(x_skip, 2 * q + a + 1, r, value)
                total = value if total is None else total + value
            halves = []
            for k in range(ch // 128):
                pair[r, k] = total[:, k * 128 : (k + 1) * 128]
                even = pair[r, k, pl.ds(0, cc, stride=2), :]
                odd = pair[r, k, pl.ds(1, cc, stride=2), :]
                halves.append((even + odd) * 0.25)
            spread(x_pool, q + 1, r, jnp.concatenate(halves, axis=1).astype(BF16).astype(F32))

    pool = Exchange(1, x_pool, halo_pool, edges_pool, recv_pool)
    skip = Exchange(2, x_skip, halo.at[1], edges.at[1], recv_skip)
    pool.prepare()
    pool.send()
    skip.prepare()
    loads[2].wait()
    inner_rows(x_skip, acc_dec, dec_weights(1), 0, 1, False)
    pool.relay()
    inner_rows(x_skip, acc_dec, dec_weights(1), 1, inner, False)
    skip.send()

    loads[3].wait()
    loads[4].wait()
    pool.wait_rows()

    acc_mid = acc_enc.at[0:hc, :, 0:cc, :]

    @pl.loop(0, hc // 2)
    def _(k):
        acc_enc[pl.ds(2 * k, 2), :, 0:cc, :] = conv_rows(x_pool, 2 * k, 2, mid_weights)

    pool.add_seams(acc_mid, lambda a, b: mid_w[a, b])

    @pl.loop(0, hc)
    def _(q):
        for r in range(cycles):
            value = gelu_tanh(acc_enc[q, r, 0:cc, :] + mid_b[...])
            coarse[q, r] = value.astype(BF16)

    @pl.loop(0, hc)
    def _(q):
        lhs = coarse[q].reshape(cycles * cc, ch)
        for a in range(2):
            for b in range(2):
                value = jnp.dot(lhs, up_w[a, b], preferred_element_type=F32) + up_b[...]
                for r in range(cycles):
                    for k in range(ch // 128):
                        fine[a, r, k, pl.ds(b, cc, stride=2), :] = value[
                            r * cc : (r + 1) * cc, k * 128 : (k + 1) * 128
                        ]
            for r in range(cycles):
                row = jnp.concatenate([fine[a, r, k] for k in range(ch // 128)], axis=1)
                spread(x_up, 2 * q + a + 1, r, row.astype(BF16).astype(F32))

    up = Exchange(3, x_up, halo.at[2], edges.at[2], recv_up)
    up.prepare()
    up.send()
    skip.relay()
    skip.wait_rows()
    outer_rows(x_skip, acc_dec, dec_weights(1), False)
    up.relay()
    inner_rows(x_up, acc_dec, dec_weights(0), 0, inner, True)
    skip.add_seams(acc_dec, dec_tap(1))
    up.wait_rows()
    outer_rows(x_up, acc_dec, dec_weights(0), True)
    up.add_seams(acc_dec, dec_tap(0))

    @pl.loop(0, h)
    def _(i):
        for r in range(cycles):
            out[r, i] = (acc_dec[i, r] + dec_b[...]).astype(BF16)


def solution(mesh):
    tiles = mesh.shape["tile"]

    def on_device(fields, seam_tile, seam_code, enc_w, enc_b, mid_w, mid_b, up_w, up_b, dec_w, dec_b):
        cycles, h, cols, ch = fields.shape
        hc, cc = h // 2, cols // 2
        vmem = pl.BlockSpec(memory_space=pltpu.VMEM)
        smem = pl.BlockSpec(memory_space=pltpu.SMEM)
        hbm = pl.BlockSpec(memory_space=pl.ANY)
        ends = 2 * cycles
        slots = 2 * FACES
        return pl.pallas_call(
            functools.partial(kernel, tiles),
            out_shape=jax.ShapeDtypeStruct(fields.shape, BF16),
            in_specs=[smem, smem] + [hbm] * 5 + [vmem] * 4,
            out_specs=vmem,
            scratch_shapes=[
                pltpu.VMEM(fields.shape, BF16),
                pltpu.VMEM(enc_w.shape, BF16),
                pltpu.VMEM(mid_w.shape, BF16),
                pltpu.VMEM(up_w.shape, BF16),
                pltpu.VMEM(dec_w.shape, BF16),
                pltpu.VMEM((h + 2, cycles, cols, 3 * ch), BF16),
                pltpu.VMEM((h + 2, cycles, cols, 3 * ch), BF16),
                pltpu.VMEM((hc + 2, cycles, cc, 3 * ch), BF16),
                pltpu.VMEM((h + 2, cycles, cols, 3 * ch), BF16),
                pltpu.VMEM((h, cycles, cols, ch), F32),
                pltpu.VMEM((h, cycles, cols, ch), F32),
                pltpu.VMEM((hc, cycles, cc, ch), BF16),
                pltpu.VMEM((2, cycles, ch // 128, cols, 128), F32),
                pltpu.VMEM((cycles, ch // 128, cols, 128), F32),
                pltpu.VMEM((4, 2, 8, ch), F32),
                pltpu.VMEM((4, ends, 8, ch), F32),
                pltpu.VMEM((2, cycles, 16, ch), F32),
                pltpu.VMEM((4, 2, 8, ch), BF16),
                pltpu.VMEM((4, 2, 8, ch), BF16),
                pltpu.VMEM((4, 16, ch), BF16),
                pltpu.VMEM((3, 2, cycles, cols, ch), BF16),
                pltpu.VMEM((2, cycles, cc, ch), BF16),
                pltpu.VMEM((3, ends, h, ch), BF16),
                pltpu.VMEM((ends, hc, ch), BF16),
                pltpu.VMEM((slots, ends, h, ch), BF16),
                pltpu.VMEM((slots, ends, h, ch), BF16),
                pltpu.VMEM((slots, ends, h, ch), BF16),
                pltpu.VMEM((slots, ends, hc, ch), BF16),
                pltpu.VMEM((slots, 16, ch), BF16),
                pltpu.VMEM((slots, 16, ch), BF16),
                pltpu.VMEM((slots, 16, ch), BF16),
                pltpu.VMEM((slots, 16, ch), BF16),
                pltpu.SemaphoreType.DMA((5,)),
                pltpu.SemaphoreType.DMA((4, 4 + 2 * slots)),
                pltpu.SemaphoreType.DMA((4, 4 + 2 * slots)),
            ],
            compiler_params=pltpu.CompilerParams(
                collective_id=0, has_side_effects=True, vmem_limit_bytes=60 * 1024 * 1024
            ),
        )(
            seam_tile.reshape(cycles, 2),
            seam_code.reshape(cycles, 2),
            fields,
            enc_w,
            mid_w,
            up_w,
            dec_w,
            enc_b.reshape(1, ch),
            mid_b.reshape(1, ch),
            up_b.reshape(1, ch),
            dec_b.reshape(1, ch),
        )

    return jax.shard_map(
        on_device,
        mesh=mesh,
        in_specs=(P("grp", "tile", None, None), P(None, "tile", None), P(None, "tile", None)) + (P(),) * 8,
        out_specs=P("grp", "tile", None, None),
        check_vma=False,
    )
```

```python
import functools

import jax
import jax.numpy as jnp
from jax import lax
from jax.experimental import pallas as pl
from jax.experimental.pallas import tpu as pltpu
from jax.sharding import PartitionSpec as P

F32 = jnp.float32
BF16 = jnp.bfloat16
FACES = 4


def gelu_tanh(x):
    return 0.5 * x * (1.0 + jnp.tanh(0.7978845608 * (x + 0.044715 * (x * x * x))))


def kernel(
    tiles,
    seam_tile,
    seam_code,
    fields_hbm,
    enc_w_hbm,
    mid_w_hbm,
    up_w_hbm,
    dec_w_hbm,
    enc_b,
    mid_b,
    up_b,
    dec_b,
    out,
    fields,
    enc_w,
    mid_w,
    up_w,
    dec_w,
    x_enc,
    x_skip,
    x_pool,
    x_up,
    acc_enc,
    acc_dec,
    coarse,
    fine,
    pair,
    corner_tmp,
    edge_tmp,
    seam_tmp,
    corner_src,
    corner_dst,
    corners,
    halo,
    halo_pool,
    edges,
    edges_pool,
    recv_enc,
    recv_skip,
    recv_up,
    recv_pool,
    corner_enc,
    corner_pool,
    corner_skip,
    corner_up,
    load_sem,
    send_sem,
    recv_sem,
):
    recv_corners = (corner_enc, corner_pool, corner_skip, corner_up)
    cycles, h, cols, ch = fields.shape
    hc, cc = h // 2, cols // 2
    strips = tiles // FACES
    me = lax.axis_index("tile")
    place = lax.rem(me + strips // 2, tiles)
    face = place // strips
    strip = place - face * strips
    top_face = strip == 0
    bottom_face = strip == strips - 1
    up_tile = lax.rem(me + tiles - 1, tiles)
    down_tile = lax.rem(me + 1, tiles)

    def tile_of(f, s):
        return lax.rem(f * strips + s + tiles - strips // 2, tiles)

    peers = []
    for kind in range(2):
        s = strip if kind == 0 else strips - 1 - strip
        for j in range(1 - kind, FACES):
            f = lax.rem(face + j, FACES)
            peers.append((kind, f, tile_of(f, s)))

    loads = []
    for k, (src, dst) in enumerate(
        ((fields_hbm, fields), (enc_w_hbm, enc_w), (dec_w_hbm, dec_w), (mid_w_hbm, mid_w), (up_w_hbm, up_w))
    ):
        copy = pltpu.make_async_copy(src, dst, load_sem.at[k])
        copy.start()
        loads.append(copy)

    barrier = pltpu.get_barrier_semaphore()
    targets = [up_tile, down_tile] + [peer for _, _, peer in peers]
    for target in targets:
        pl.semaphore_signal(barrier, inc=1, device_id={"tile": target})

    def remote(src, dst, e, send_at, recv_at, target):
        return pltpu.make_async_remote_copy(
            src_ref=src,
            dst_ref=dst,
            send_sem=send_sem.at[e, send_at],
            recv_sem=recv_sem.at[e, recv_at],
            device_id={"tile": target},
        )

    def spread(x, i, r, value):
        width = value.shape[0]
        at = lax.broadcasted_iota(jnp.int32, value.shape, 0)
        left = jnp.where(at == 0, 0.0, pltpu.roll(value, 1, 0))
        right = jnp.where(at == width - 1, 0.0, pltpu.roll(value, width - 1, 0))
        x[i, r, :, 0:ch] = left.astype(BF16)
        x[i, r, :, ch : 2 * ch] = value.astype(BF16)
        x[i, r, :, 2 * ch : 3 * ch] = right.astype(BF16)

    class Exchange:
        def __init__(self, e, x, halo_ref, edge_ref, recv_ref, source=None):
            self.e, self.x, self.halo, self.edges, self.recv = e, x, halo_ref, edge_ref, recv_ref
            self.rows = x.shape[0] - 2
            self.width = x.shape[2]
            self.source = source

        def row(self, i):
            if self.source is None:
                return self.x.at[i + 1, :, :, ch : 2 * ch]
            return self.source.at[:, i]

        def end_pixels(self, i, r):
            row = self.row(i)
            head = row[r, 0:16, :].astype(F32)[0:1]
            tail = row[r, self.width - 16 : self.width, :].astype(F32)[15:16]
            return head, tail

        def prepare(self):
            e, rows = self.e, self.rows
            for r in range(cycles):
                for i in range(rows):
                    for side, pixel in enumerate(self.end_pixels(i, r)):
                        k = 2 * r + side
                        edge_tmp[e, k, i : i + 1, :] = pixel
                        if i == 0:
                            corner_tmp[e, 0, k : k + 1, :] = pixel
                        if i == rows - 1:
                            corner_tmp[e, 1, k : k + 1, :] = pixel
            for which in range(2):
                corner_src[e, which] = corner_tmp[e, which].astype(BF16)
            value = edge_tmp[e, :, 0:rows, :].astype(BF16)
            self.edges[...] = value
            self.recv[face] = value

        def send(self):
            e, rows = self.e, self.rows
            self.copies = [
                remote(corner_src.at[e, 1], corner_dst.at[e, 0], e, 0, 0, down_tile),
                remote(corner_src.at[e, 0], corner_dst.at[e, 1], e, 1, 1, up_tile),
                remote(self.row(rows - 1), self.halo.at[0], e, 2, 2, down_tile),
                remote(self.row(0), self.halo.at[1], e, 3, 3, up_tile),
            ]
            self.seams = [
                remote(
                    self.edges,
                    self.recv.at[kind * FACES + face],
                    e,
                    4 + kind * FACES + f,
                    4 + kind * FACES + face,
                    peer,
                )
                for kind, f, peer in peers
            ]
            for copy in self.copies[0:2] + self.seams + self.copies[2:4]:
                copy.start()

        def relay(self):
            e = self.e
            self.copies[0].wait_recv()
            self.copies[1].wait_recv()
            above = jnp.where(top_face, 0.0, corner_dst[e, 0].astype(F32))
            below = jnp.where(bottom_face, 0.0, corner_dst[e, 1].astype(F32))
            value = jnp.concatenate([above, below], axis=0).astype(BF16)
            corners[e] = value
            self.recv_corner = recv_corners[e]
            self.recv_corner[face] = value
            self.relays = [
                remote(
                    corners.at[e],
                    self.recv_corner.at[kind * FACES + face],
                    e,
                    12 + kind * FACES + f,
                    12 + kind * FACES + face,
                    peer,
                )
                for kind, f, peer in peers
            ]
            for copy in self.relays:
                copy.start()

        def wait_rows(self):
            self.copies[2].wait_recv()
            self.copies[3].wait_recv()
            for r in range(cycles):
                above = jnp.where(top_face, 0.0, self.halo[0, r].astype(F32))
                spread(self.x, 0, r, above)
                below = jnp.where(bottom_face, 0.0, self.halo[1, r].astype(F32))
                spread(self.x, self.rows + 1, r, below)

        def wait_seams(self):
            e = self.e
            for kind, f, peer in peers:
                slot = kind * FACES + f
                remote(self.edges, self.recv.at[slot], e, 4 + slot, 4 + slot, peer).wait_recv()
                remote(
                    corners.at[e], self.recv_corner.at[slot], e, 12 + slot, 12 + slot, peer
                ).wait_recv()
            for copy in self.copies + self.seams + self.relays:
                copy.wait_send()

        def load_seams(self):
            rows = self.rows
            at = lax.broadcasted_iota(jnp.int32, (8, ch), 0)
            for side in range(2):
                for r in range(cycles):
                    partner, code = seam_tile[r, side], seam_code[r, side]
                    cycle = partner // tiles
                    home = lax.rem(partner - cycle * tiles + strips // 2, tiles) // strips
                    mirrored = code >= 2
                    slot = jnp.where(mirrored, FACES, 0) + home
                    k = 2 * cycle + lax.rem(code, 2)
                    column = self.recv[slot, k].astype(F32)
                    ends = self.recv_corner[slot].astype(F32)
                    above = jnp.sum(jnp.where(at == k, ends[0:8], 0.0), axis=0, keepdims=True)
                    below = jnp.sum(jnp.where(at == k, ends[8:16], 0.0), axis=0, keepdims=True)
                    seam_tmp[side, r, 0:1, :] = jnp.where(mirrored, below, above)
                    seam_tmp[side, r, rows + 1 : rows + 2, :] = jnp.where(mirrored, above, below)
                    for i in range(rows):
                        seam_tmp[side, r, i + 1 : i + 2, :] = jnp.where(
                            mirrored, column[rows - 1 - i : rows - i], column[i : i + 1]
                        )

        def add_seams(self, acc, weight_of):
            self.wait_seams()
            self.load_seams()
            for side in range(2):
                j = 0 if side == 0 else self.width - 1
                term = jnp.zeros((8 * cycles, ch), F32)
                for a in range(3):
                    tap = jnp.concatenate([seam_tmp[side, r, a : a + 8, :] for r in range(cycles)], axis=0)
                    term = term + jnp.dot(tap.astype(BF16), weight_of(a, 2 * side), preferred_element_type=F32)
                for r in range(cycles):
                    for i in range(self.rows):
                        acc[i, r, j : j + 1, :] += term[8 * r + i : 8 * r + i + 1]

    def conv_rows(x, start, count, weights):
        width = x.shape[2]
        taps = [x[pl.ds(start + a, count)].reshape(count * cycles * width, 3 * ch) for a in range(3)]
        product = jnp.dot(jnp.concatenate(taps, axis=1), weights(), preferred_element_type=F32)
        return product.reshape(count, cycles, width, ch)

    def enc_weights():
        return enc_w[...].reshape(9 * ch, ch)

    def mid_weights():
        return mid_w[...].reshape(9 * ch, ch)

    def dec_weights(part):
        def get():
            picked = [dec_w[a, b, part * ch : (part + 1) * ch, :] for a in range(3) for b in range(3)]
            return jnp.concatenate(picked, axis=0)

        return get

    def dec_tap(part):
        return lambda a, b: dec_w[a, b, part * ch : (part + 1) * ch, :]

    loads[0].wait()
    enc = Exchange(0, x_enc, halo.at[0], edges.at[0], recv_enc, fields)
    enc.prepare()
    @pl.loop(0, h)
    def _(i):
        for r in range(cycles):
            spread(x_enc, i + 1, r, fields[r, i].astype(F32))

    pl.semaphore_wait(barrier, len(targets))
    enc.send()

    loads[1].wait()

    def inner_rows(x, acc, weights, lo, hi, add):
        @pl.loop(lo, hi)
        def _(k):
            start = 1 + 2 * k
            value = conv_rows(x, start, 2, weights)
            if add:
                acc[pl.ds(start, 2)] += value
            else:
                acc[pl.ds(start, 2)] = value

    inner = (h - 2) // 2

    def outer_rows(x, acc, weights, add):
        @pl.loop(0, 2)
        def _(k):
            i = k * (h - 1)
            value = conv_rows(x, i, 1, weights)
            if add:
                acc[pl.ds(i, 1)] += value
            else:
                acc[pl.ds(i, 1)] = value

    inner_rows(x_enc, acc_enc, enc_weights, 0, 1, False)
    enc.relay()
    inner_rows(x_enc, acc_enc, enc_weights, 1, inner, False)
    enc.wait_rows()
    outer_rows(x_enc, acc_enc, enc_weights, False)
    enc.add_seams(acc_enc, lambda a, b: enc_w[a, b])

    @pl.loop(0, hc)
    def _(q):
        for r in range(cycles):
            total = None
            for a in range(2):
                value = gelu_tanh(acc_enc[2 * q + a, r] + enc_b[...]).astype(BF16).astype(F32)
                spread(x_skip, 2 * q + a + 1, r, value)
                total = value if total is None else total + value
            halves = []
            for k in range(ch // 128):
                pair[r, k] = total[:, k * 128 : (k + 1) * 128]
                even = pair[r, k, pl.ds(0, cc, stride=2), :]
                odd = pair[r, k, pl.ds(1, cc, stride=2), :]
                halves.append((even + odd) * 0.25)
            spread(x_pool, q + 1, r, jnp.concatenate(halves, axis=1).astype(BF16).astype(F32))

    pool = Exchange(1, x_pool, halo_pool, edges_pool, recv_pool)
    skip = Exchange(2, x_skip, halo.at[1], edges.at[1], recv_skip)
    pool.prepare()
    pool.send()
    skip.prepare()
    loads[2].wait()
    inner_rows(x_skip, acc_dec, dec_weights(1), 0, 1, False)
    pool.relay()
    inner_rows(x_skip, acc_dec, dec_weights(1), 1, inner, False)
    skip.send()

    loads[3].wait()
    loads[4].wait()
    pool.wait_rows()

    acc_mid = acc_enc.at[0:hc, :, 0:cc, :]

    @pl.loop(0, hc // 2)
    def _(k):
        acc_enc[pl.ds(2 * k, 2), :, 0:cc, :] = conv_rows(x_pool, 2 * k, 2, mid_weights)

    skip.relay()
    pool.add_seams(acc_mid, lambda a, b: mid_w[a, b])

    @pl.loop(0, hc)
    def _(q):
        for r in range(cycles):
            value = gelu_tanh(acc_enc[q, r, 0:cc, :] + mid_b[...])
            coarse[q, r] = value.astype(BF16)

    @pl.loop(0, hc)
    def _(q):
        lhs = coarse[q].reshape(cycles * cc, ch)
        for a in range(2):
            for b in range(2):
                value = jnp.dot(lhs, up_w[a, b], preferred_element_type=F32) + up_b[...]
                for r in range(cycles):
                    for k in range(ch // 128):
                        fine[a, r, k, pl.ds(b, cc, stride=2), :] = value[
                            r * cc : (r + 1) * cc, k * 128 : (k + 1) * 128
                        ]
            for r in range(cycles):
                row = jnp.concatenate([fine[a, r, k] for k in range(ch // 128)], axis=1)
                spread(x_up, 2 * q + a + 1, r, row.astype(BF16).astype(F32))

    up = Exchange(3, x_up, halo.at[2], edges.at[2], recv_up)
    up.prepare()
    up.send()
    skip.wait_rows()
    outer_rows(x_skip, acc_dec, dec_weights(1), False)
    up.relay()
    inner_rows(x_up, acc_dec, dec_weights(0), 0, inner, True)
    skip.add_seams(acc_dec, dec_tap(1))
    up.wait_rows()
    outer_rows(x_up, acc_dec, dec_weights(0), True)
    up.add_seams(acc_dec, dec_tap(0))

    @pl.loop(0, h)
    def _(i):
        for r in range(cycles):
            out[r, i] = (acc_dec[i, r] + dec_b[...]).astype(BF16)


def solution(mesh):
    tiles = mesh.shape["tile"]

    def on_device(fields, seam_tile, seam_code, enc_w, enc_b, mid_w, mid_b, up_w, up_b, dec_w, dec_b):
        cycles, h, cols, ch = fields.shape
        hc, cc = h // 2, cols // 2
        vmem = pl.BlockSpec(memory_space=pltpu.VMEM)
        smem = pl.BlockSpec(memory_space=pltpu.SMEM)
        hbm = pl.BlockSpec(memory_space=pl.ANY)
        ends = 2 * cycles
        slots = 2 * FACES
        return pl.pallas_call(
            functools.partial(kernel, tiles),
            out_shape=jax.ShapeDtypeStruct(fields.shape, BF16),
            in_specs=[smem, smem] + [hbm] * 5 + [vmem] * 4,
            out_specs=vmem,
            scratch_shapes=[
                pltpu.VMEM(fields.shape, BF16),
                pltpu.VMEM(enc_w.shape, BF16),
                pltpu.VMEM(mid_w.shape, BF16),
                pltpu.VMEM(up_w.shape, BF16),
                pltpu.VMEM(dec_w.shape, BF16),
                pltpu.VMEM((h + 2, cycles, cols, 3 * ch), BF16),
                pltpu.VMEM((h + 2, cycles, cols, 3 * ch), BF16),
                pltpu.VMEM((hc + 2, cycles, cc, 3 * ch), BF16),
                pltpu.VMEM((h + 2, cycles, cols, 3 * ch), BF16),
                pltpu.VMEM((h, cycles, cols, ch), F32),
                pltpu.VMEM((h, cycles, cols, ch), F32),
                pltpu.VMEM((hc, cycles, cc, ch), BF16),
                pltpu.VMEM((2, cycles, ch // 128, cols, 128), F32),
                pltpu.VMEM((cycles, ch // 128, cols, 128), F32),
                pltpu.VMEM((4, 2, 8, ch), F32),
                pltpu.VMEM((4, ends, 8, ch), F32),
                pltpu.VMEM((2, cycles, 16, ch), F32),
                pltpu.VMEM((4, 2, 8, ch), BF16),
                pltpu.VMEM((4, 2, 8, ch), BF16),
                pltpu.VMEM((4, 16, ch), BF16),
                pltpu.VMEM((3, 2, cycles, cols, ch), BF16),
                pltpu.VMEM((2, cycles, cc, ch), BF16),
                pltpu.VMEM((3, ends, h, ch), BF16),
                pltpu.VMEM((ends, hc, ch), BF16),
                pltpu.VMEM((slots, ends, h, ch), BF16),
                pltpu.VMEM((slots, ends, h, ch), BF16),
                pltpu.VMEM((slots, ends, h, ch), BF16),
                pltpu.VMEM((slots, ends, hc, ch), BF16),
                pltpu.VMEM((slots, 16, ch), BF16),
                pltpu.VMEM((slots, 16, ch), BF16),
                pltpu.VMEM((slots, 16, ch), BF16),
                pltpu.VMEM((slots, 16, ch), BF16),
                pltpu.SemaphoreType.DMA((5,)),
                pltpu.SemaphoreType.DMA((4, 4 + 2 * slots)),
                pltpu.SemaphoreType.DMA((4, 4 + 2 * slots)),
            ],
            compiler_params=pltpu.CompilerParams(
                collective_id=0, has_side_effects=True, vmem_limit_bytes=60 * 1024 * 1024
            ),
        )(
            seam_tile.reshape(cycles, 2),
            seam_code.reshape(cycles, 2),
            fields,
            enc_w,
            mid_w,
            up_w,
            dec_w,
            enc_b.reshape(1, ch),
            mid_b.reshape(1, ch),
            up_b.reshape(1, ch),
            dec_b.reshape(1, ch),
        )

    return jax.shard_map(
        on_device,
        mesh=mesh,
        in_specs=(P("grp", "tile", None, None), P(None, "tile", None), P(None, "tile", None)) + (P(),) * 8,
        out_specs=P("grp", "tile", None, None),
        check_vma=False,
    )
```

```python
import functools

import jax
import jax.numpy as jnp
from jax import lax
from jax.experimental import pallas as pl
from jax.experimental.pallas import tpu as pltpu
from jax.sharding import PartitionSpec as P

F32 = jnp.float32
BF16 = jnp.bfloat16
FACES = 4


def gelu_tanh(x):
    return 0.5 * x * (1.0 + jnp.tanh(0.7978845608 * (x + 0.044715 * (x * x * x))))


def kernel(
    tiles,
    seam_tile,
    seam_code,
    fields_hbm,
    enc_w_hbm,
    mid_w_hbm,
    up_w_hbm,
    dec_w_hbm,
    enc_b,
    mid_b,
    up_b,
    dec_b,
    out,
    fields,
    enc_w,
    mid_w,
    up_w,
    dec_w,
    x_enc,
    x_skip,
    x_pool,
    x_up,
    acc_enc,
    acc_dec,
    coarse,
    fine,
    pair,
    corner_tmp,
    edge_tmp,
    seam_tmp,
    corner_src,
    corner_dst,
    corners,
    halo,
    halo_pool,
    edges,
    edges_pool,
    recv_enc,
    recv_skip,
    recv_up,
    recv_pool,
    corner_enc,
    corner_pool,
    corner_skip,
    corner_up,
    load_sem,
    send_sem,
    recv_sem,
):
    recv_corners = (corner_enc, corner_pool, corner_skip, corner_up)
    cycles, h, cols, ch = fields.shape
    hc, cc = h // 2, cols // 2
    strips = tiles // FACES
    me = lax.axis_index("tile")
    place = lax.rem(me + strips // 2, tiles)
    face = place // strips
    strip = place - face * strips
    top_face = strip == 0
    bottom_face = strip == strips - 1
    up_tile = lax.rem(me + tiles - 1, tiles)
    down_tile = lax.rem(me + 1, tiles)

    def tile_of(f, s):
        return lax.rem(f * strips + s + tiles - strips // 2, tiles)

    peers = []
    for kind in range(2):
        s = strip if kind == 0 else strips - 1 - strip
        for j in range(1 - kind, FACES):
            f = lax.rem(face + j, FACES)
            peers.append((kind, f, tile_of(f, s)))

    loads = []
    for k, (src, dst) in enumerate(
        ((fields_hbm, fields), (enc_w_hbm, enc_w), (dec_w_hbm, dec_w), (mid_w_hbm, mid_w), (up_w_hbm, up_w))
    ):
        copy = pltpu.make_async_copy(src, dst, load_sem.at[k])
        copy.start()
        loads.append(copy)

    barrier = pltpu.get_barrier_semaphore()
    targets = [up_tile, down_tile] + [peer for _, _, peer in peers]
    for target in targets:
        pl.semaphore_signal(barrier, inc=1, device_id={"tile": target})

    def remote(src, dst, e, send_at, recv_at, target):
        return pltpu.make_async_remote_copy(
            src_ref=src,
            dst_ref=dst,
            send_sem=send_sem.at[e, send_at],
            recv_sem=recv_sem.at[e, recv_at],
            device_id={"tile": target},
        )

    def spread(x, i, r, value):
        width = value.shape[0]
        at = lax.broadcasted_iota(jnp.int32, value.shape, 0)
        left = jnp.where(at == 0, 0.0, pltpu.roll(value, 1, 0))
        right = jnp.where(at == width - 1, 0.0, pltpu.roll(value, width - 1, 0))
        x[i, r, :, 0:ch] = left.astype(BF16)
        x[i, r, :, ch : 2 * ch] = value.astype(BF16)
        x[i, r, :, 2 * ch : 3 * ch] = right.astype(BF16)

    class Exchange:
        def __init__(self, e, x, halo_ref, edge_ref, recv_ref, source=None):
            self.e, self.x, self.halo, self.edges, self.recv = e, x, halo_ref, edge_ref, recv_ref
            self.rows = x.shape[0] - 2
            self.width = x.shape[2]
            self.source = source

        def row(self, i):
            if self.source is None:
                return self.x.at[i + 1, :, :, ch : 2 * ch]
            return self.source.at[:, i]

        def end_pixels(self, i, r):
            row = self.row(i)
            head = row[r, 0:16, :].astype(F32)[0:1]
            tail = row[r, self.width - 16 : self.width, :].astype(F32)[15:16]
            return head, tail

        def prepare(self):
            e, rows = self.e, self.rows
            for r in range(cycles):
                for i in range(rows):
                    for side, pixel in enumerate(self.end_pixels(i, r)):
                        k = 2 * r + side
                        edge_tmp[e, k, i : i + 1, :] = pixel
                        if i == 0:
                            corner_tmp[e, 0, k : k + 1, :] = pixel
                        if i == rows - 1:
                            corner_tmp[e, 1, k : k + 1, :] = pixel
            for which in range(2):
                corner_src[e, which] = corner_tmp[e, which].astype(BF16)
            value = edge_tmp[e, :, 0:rows, :].astype(BF16)
            self.edges[...] = value
            self.recv[face] = value

        def send(self):
            e, rows = self.e, self.rows
            self.copies = [
                remote(corner_src.at[e, 1], corner_dst.at[e, 0], e, 0, 0, down_tile),
                remote(corner_src.at[e, 0], corner_dst.at[e, 1], e, 1, 1, up_tile),
                remote(self.row(rows - 1), self.halo.at[0], e, 2, 2, down_tile),
                remote(self.row(0), self.halo.at[1], e, 3, 3, up_tile),
            ]
            self.seams = [
                remote(
                    self.edges,
                    self.recv.at[kind * FACES + face],
                    e,
                    4 + kind * FACES + f,
                    4 + kind * FACES + face,
                    peer,
                )
                for kind, f, peer in peers
            ]
            for copy in self.copies[0:2] + self.seams + self.copies[2:4]:
                copy.start()

        def relay(self):
            e = self.e
            self.copies[0].wait_recv()
            self.copies[1].wait_recv()
            above = jnp.where(top_face, 0.0, corner_dst[e, 0].astype(F32))
            below = jnp.where(bottom_face, 0.0, corner_dst[e, 1].astype(F32))
            value = jnp.concatenate([above, below], axis=0).astype(BF16)
            corners[e] = value
            self.recv_corner = recv_corners[e]
            self.recv_corner[face] = value
            self.relays = [
                remote(
                    corners.at[e],
                    self.recv_corner.at[kind * FACES + face],
                    e,
                    12 + kind * FACES + f,
                    12 + kind * FACES + face,
                    peer,
                )
                for kind, f, peer in peers
            ]
            for copy in self.relays:
                copy.start()

        def wait_rows(self):
            self.copies[2].wait_recv()
            self.copies[3].wait_recv()
            for r in range(cycles):
                above = jnp.where(top_face, 0.0, self.halo[0, r].astype(F32))
                spread(self.x, 0, r, above)
                below = jnp.where(bottom_face, 0.0, self.halo[1, r].astype(F32))
                spread(self.x, self.rows + 1, r, below)

        def wait_seams(self):
            e = self.e
            for kind, f, peer in peers:
                slot = kind * FACES + f
                remote(self.edges, self.recv.at[slot], e, 4 + slot, 4 + slot, peer).wait_recv()
                remote(
                    corners.at[e], self.recv_corner.at[slot], e, 12 + slot, 12 + slot, peer
                ).wait_recv()
            for copy in self.copies + self.seams + self.relays:
                copy.wait_send()

        def load_seams(self):
            rows = self.rows
            at = lax.broadcasted_iota(jnp.int32, (8, ch), 0)
            for side in range(2):
                for r in range(cycles):
                    partner, code = seam_tile[r, side], seam_code[r, side]
                    cycle = partner // tiles
                    home = lax.rem(partner - cycle * tiles + strips // 2, tiles) // strips
                    mirrored = code >= 2
                    slot = jnp.where(mirrored, FACES, 0) + home
                    k = 2 * cycle + lax.rem(code, 2)
                    column = self.recv[slot, k].astype(F32)
                    ends = self.recv_corner[slot].astype(F32)
                    above = jnp.sum(jnp.where(at == k, ends[0:8], 0.0), axis=0, keepdims=True)
                    below = jnp.sum(jnp.where(at == k, ends[8:16], 0.0), axis=0, keepdims=True)
                    seam_tmp[side, r, 0:1, :] = jnp.where(mirrored, below, above)
                    seam_tmp[side, r, rows + 1 : rows + 2, :] = jnp.where(mirrored, above, below)
                    for i in range(rows):
                        seam_tmp[side, r, i + 1 : i + 2, :] = jnp.where(
                            mirrored, column[rows - 1 - i : rows - i], column[i : i + 1]
                        )

        def add_seams(self, acc, weight_of):
            self.wait_seams()
            self.load_seams()
            for side in range(2):
                j = 0 if side == 0 else self.width - 1
                term = jnp.zeros((8 * cycles, ch), F32)
                for a in range(3):
                    tap = jnp.concatenate([seam_tmp[side, r, a : a + 8, :] for r in range(cycles)], axis=0)
                    term = term + jnp.dot(tap.astype(BF16), weight_of(a, 2 * side), preferred_element_type=F32)
                for r in range(cycles):
                    for i in range(self.rows):
                        acc[i, r, j : j + 1, :] += term[8 * r + i : 8 * r + i + 1]

    def conv_rows(x, start, count, weights):
        width = x.shape[2]
        taps = [x[pl.ds(start + a, count)].reshape(count * cycles * width, 3 * ch) for a in range(3)]
        product = jnp.dot(jnp.concatenate(taps, axis=1), weights(), preferred_element_type=F32)
        return product.reshape(count, cycles, width, ch)

    def enc_weights():
        return enc_w[...].reshape(9 * ch, ch)

    def mid_weights():
        return mid_w[...].reshape(9 * ch, ch)

    def dec_weights(part):
        def get():
            picked = [dec_w[a, b, part * ch : (part + 1) * ch, :] for a in range(3) for b in range(3)]
            return jnp.concatenate(picked, axis=0)

        return get

    def dec_tap(part):
        return lambda a, b: dec_w[a, b, part * ch : (part + 1) * ch, :]

    loads[0].wait()
    enc = Exchange(0, x_enc, halo.at[0], edges.at[0], recv_enc, fields)
    enc.prepare()
    @pl.loop(0, h)
    def _(i):
        for r in range(cycles):
            spread(x_enc, i + 1, r, fields[r, i].astype(F32))

    pl.semaphore_wait(barrier, len(targets))
    enc.send()

    loads[1].wait()

    def inner_rows(x, acc, weights, lo, hi, add):
        @pl.loop(lo, hi)
        def _(k):
            start = 1 + 2 * k
            value = conv_rows(x, start, 2, weights)
            if add:
                acc[pl.ds(start, 2)] += value
            else:
                acc[pl.ds(start, 2)] = value

    inner = (h - 2) // 2

    def outer_rows(x, acc, weights, add):
        @pl.loop(0, 2)
        def _(k):
            i = k * (h - 1)
            value = conv_rows(x, i, 1, weights)
            if add:
                acc[pl.ds(i, 1)] += value
            else:
                acc[pl.ds(i, 1)] = value

    inner_rows(x_enc, acc_enc, enc_weights, 0, 1, False)
    enc.relay()
    inner_rows(x_enc, acc_enc, enc_weights, 1, inner, False)
    enc.wait_rows()
    outer_rows(x_enc, acc_enc, enc_weights, False)
    enc.add_seams(acc_enc, lambda a, b: enc_w[a, b])

    @pl.loop(0, hc)
    def _(q):
        for r in range(cycles):
            total = None
            for a in range(2):
                value = gelu_tanh(acc_enc[2 * q + a, r] + enc_b[...]).astype(BF16).astype(F32)
                spread(x_skip, 2 * q + a + 1, r, value)
                total = value if total is None else total + value
            halves = []
            for k in range(ch // 128):
                pair[r, k] = total[:, k * 128 : (k + 1) * 128]
                even = pair[r, k, pl.ds(0, cc, stride=2), :]
                odd = pair[r, k, pl.ds(1, cc, stride=2), :]
                halves.append((even + odd) * 0.25)
            spread(x_pool, q + 1, r, jnp.concatenate(halves, axis=1).astype(BF16).astype(F32))

    pool = Exchange(1, x_pool, halo_pool, edges_pool, recv_pool)
    skip = Exchange(2, x_skip, halo.at[1], edges.at[1], recv_skip)
    pool.prepare()
    pool.send()
    skip.prepare()
    loads[2].wait()
    inner_rows(x_skip, acc_dec, dec_weights(1), 0, 1, False)
    pool.relay()
    skip.send()
    inner_rows(x_skip, acc_dec, dec_weights(1), 1, inner, False)

    loads[3].wait()
    loads[4].wait()
    pool.wait_rows()

    acc_mid = acc_enc.at[0:hc, :, 0:cc, :]

    @pl.loop(0, hc // 2)
    def _(k):
        acc_enc[pl.ds(2 * k, 2), :, 0:cc, :] = conv_rows(x_pool, 2 * k, 2, mid_weights)

    skip.relay()
    pool.add_seams(acc_mid, lambda a, b: mid_w[a, b])

    @pl.loop(0, hc)
    def _(q):
        for r in range(cycles):
            value = gelu_tanh(acc_enc[q, r, 0:cc, :] + mid_b[...])
            coarse[q, r] = value.astype(BF16)

    @pl.loop(0, hc)
    def _(q):
        lhs = coarse[q].reshape(cycles * cc, ch)
        for a in range(2):
            for b in range(2):
                value = jnp.dot(lhs, up_w[a, b], preferred_element_type=F32) + up_b[...]
                for r in range(cycles):
                    for k in range(ch // 128):
                        fine[a, r, k, pl.ds(b, cc, stride=2), :] = value[
                            r * cc : (r + 1) * cc, k * 128 : (k + 1) * 128
                        ]
            for r in range(cycles):
                row = jnp.concatenate([fine[a, r, k] for k in range(ch // 128)], axis=1)
                spread(x_up, 2 * q + a + 1, r, row.astype(BF16).astype(F32))

    up = Exchange(3, x_up, halo.at[2], edges.at[2], recv_up)
    up.prepare()
    up.send()
    skip.wait_rows()
    outer_rows(x_skip, acc_dec, dec_weights(1), False)
    up.relay()
    inner_rows(x_up, acc_dec, dec_weights(0), 0, inner, True)
    skip.add_seams(acc_dec, dec_tap(1))
    up.wait_rows()
    outer_rows(x_up, acc_dec, dec_weights(0), True)
    up.add_seams(acc_dec, dec_tap(0))

    @pl.loop(0, h)
    def _(i):
        for r in range(cycles):
            out[r, i] = (acc_dec[i, r] + dec_b[...]).astype(BF16)


def solution(mesh):
    tiles = mesh.shape["tile"]

    def on_device(fields, seam_tile, seam_code, enc_w, enc_b, mid_w, mid_b, up_w, up_b, dec_w, dec_b):
        cycles, h, cols, ch = fields.shape
        hc, cc = h // 2, cols // 2
        vmem = pl.BlockSpec(memory_space=pltpu.VMEM)
        smem = pl.BlockSpec(memory_space=pltpu.SMEM)
        hbm = pl.BlockSpec(memory_space=pl.ANY)
        ends = 2 * cycles
        slots = 2 * FACES
        return pl.pallas_call(
            functools.partial(kernel, tiles),
            out_shape=jax.ShapeDtypeStruct(fields.shape, BF16),
            in_specs=[smem, smem] + [hbm] * 5 + [vmem] * 4,
            out_specs=vmem,
            scratch_shapes=[
                pltpu.VMEM(fields.shape, BF16),
                pltpu.VMEM(enc_w.shape, BF16),
                pltpu.VMEM(mid_w.shape, BF16),
                pltpu.VMEM(up_w.shape, BF16),
                pltpu.VMEM(dec_w.shape, BF16),
                pltpu.VMEM((h + 2, cycles, cols, 3 * ch), BF16),
                pltpu.VMEM((h + 2, cycles, cols, 3 * ch), BF16),
                pltpu.VMEM((hc + 2, cycles, cc, 3 * ch), BF16),
                pltpu.VMEM((h + 2, cycles, cols, 3 * ch), BF16),
                pltpu.VMEM((h, cycles, cols, ch), F32),
                pltpu.VMEM((h, cycles, cols, ch), F32),
                pltpu.VMEM((hc, cycles, cc, ch), BF16),
                pltpu.VMEM((2, cycles, ch // 128, cols, 128), F32),
                pltpu.VMEM((cycles, ch // 128, cols, 128), F32),
                pltpu.VMEM((4, 2, 8, ch), F32),
                pltpu.VMEM((4, ends, 8, ch), F32),
                pltpu.VMEM((2, cycles, 16, ch), F32),
                pltpu.VMEM((4, 2, 8, ch), BF16),
                pltpu.VMEM((4, 2, 8, ch), BF16),
                pltpu.VMEM((4, 16, ch), BF16),
                pltpu.VMEM((3, 2, cycles, cols, ch), BF16),
                pltpu.VMEM((2, cycles, cc, ch), BF16),
                pltpu.VMEM((3, ends, h, ch), BF16),
                pltpu.VMEM((ends, hc, ch), BF16),
                pltpu.VMEM((slots, ends, h, ch), BF16),
                pltpu.VMEM((slots, ends, h, ch), BF16),
                pltpu.VMEM((slots, ends, h, ch), BF16),
                pltpu.VMEM((slots, ends, hc, ch), BF16),
                pltpu.VMEM((slots, 16, ch), BF16),
                pltpu.VMEM((slots, 16, ch), BF16),
                pltpu.VMEM((slots, 16, ch), BF16),
                pltpu.VMEM((slots, 16, ch), BF16),
                pltpu.SemaphoreType.DMA((5,)),
                pltpu.SemaphoreType.DMA((4, 4 + 2 * slots)),
                pltpu.SemaphoreType.DMA((4, 4 + 2 * slots)),
            ],
            compiler_params=pltpu.CompilerParams(
                collective_id=0, has_side_effects=True, vmem_limit_bytes=60 * 1024 * 1024
            ),
        )(
            seam_tile.reshape(cycles, 2),
            seam_code.reshape(cycles, 2),
            fields,
            enc_w,
            mid_w,
            up_w,
            dec_w,
            enc_b.reshape(1, ch),
            mid_b.reshape(1, ch),
            up_b.reshape(1, ch),
            dec_b.reshape(1, ch),
        )

    return jax.shard_map(
        on_device,
        mesh=mesh,
        in_specs=(P("grp", "tile", None, None), P(None, "tile", None), P(None, "tile", None)) + (P(),) * 8,
        out_specs=P("grp", "tile", None, None),
        check_vma=False,
    )
```
